32 devices in a mesh: frame: 8 (over z, y), head: 2 (over x), batch: 2 (over core).
Axes of the slice: x: 2, y: 2, z: 4, core: 2. Of those that a mesh axis runs over, the one named last changes fastest.
Arguments:
- tokens: bfloat16 [8192, 1536], P(('batch', 'frame')), parts along dimension 0, may hold values from -6 to 6
- query_weight: bfloat16 [1536, 1536], P(None, 'head'), may hold values from -0.15625 to 0.15625
- key_weight: bfloat16 [1536, 1536], P(None, 'head'), may hold values from -0.15625 to 0.15625
- value_weight: bfloat16 [1536, 1536], P(None, 'head'), may hold values from -0.15625 to 0.15625
- out_weight: bfloat16 [1536, 1536], P('head'), may hold values from -0.625 to 0.625
- block_mask: int32 [16, 4, 13], P(('batch', 'frame')), parts along dimension 0, may hold values from 0 to 1, as said below
- frame_level: int32 [64], P(('batch', 'frame')), parts along dimension 0, may hold values from 0 to 15
- modulation: float32 [16, 2, 1536], replicated, may hold values from -1.2 to 13
Outputs:
- layer_out: bfloat16 [8192, 1536], P(('batch', 'frame'), 'head'), parts along dimension 0
The draws below stay inside these ranges and needn't reach their ends.
There are 2 independent parts, one for each index of `batch`. The reference program is written for one: setup_inputs(seed, part) draws one part's arguments, and reference() takes and returns one part's arrays. A program takes and returns all parts, laid end to end along the dimension named above; an argument that names none is the same for every part. Nothing has to cross between parts.
Inputs may be any that keep to these rules, and one draw needn't show every extreme that they name: `block_mask`: in span c every tile with key block below 1, and the tile of query block i with key block (1152) / 128 + i, is always 1; the share of the other tiles that are 1 differs from span to span.
All inputs are finite; a program needn't handle non-finite values.
Results may differ from the reference program's by a relative error of at most 0.01.
The reference program's roundings to bfloat16 on the way count: a program that leaves them out, or rounds other values in their place, can miss the bound.
Values may be sent and summed in bfloat16 or wider, within the bound.
A program may use at most 128 MiB of HBM per device.

```python
import math
import jax
import jax.numpy as jnp
from jax import lax

D = 1536
HEADS = 12
HEAD_DIM = 128
SPAN = 512
FRAME_TOK = 128
SINK = 128
TILE = 128
LEVELS = 16
SPANS = 8
TOKENS = 4096
FRAMES = 32
KEYS = 1664
QBLOCKS = 4
KBLOCKS = 13


def draw_block_mask(key, part):
    first_key, second_key = jax.random.split(key)
    density = jax.random.randint(first_key, (SPANS, 1, 1), 3, 11)
    rolled = jax.random.randint(second_key, (SPANS, QBLOCKS, KBLOCKS), 0, 10)
    tile_bits = rolled < density
    diagonal = jnp.arange(KBLOCKS)[None, :] == (SINK + 2 * SPAN) // TILE + jnp.arange(QBLOCKS)[:, None]
    sink_cols = jnp.broadcast_to(jnp.arange(KBLOCKS)[None, :] < SINK // TILE, (QBLOCKS, KBLOCKS))
    return (tile_bits | diagonal[None] | sink_cols[None]).astype(jnp.int32)


def draw_modulation(key, part):
    first_key = jax.random.fold_in(key, 0)
    table_values = jnp.clip(0.3 * jax.random.normal(first_key, (LEVELS, 2, D), jnp.float32), -1.2, 1.2)
    return table_values.astype(jnp.float32)


def plant(result, rng, least, top_value):
    dims = result.shape
    index_at = [jax.random.randint(jax.random.fold_in(rng, axis), (), 0, dims[axis]) for axis in range(len(dims))]
    result = result.at[tuple(index_at)].set(least)
    longest = dims.index(max(dims))
    index_at[longest] = (index_at[longest] + 1) % dims[longest]
    return result.at[tuple(index_at)].set(top_value)


def levels(own_key, shape, cuts, smallest, top_value):
    level, own = 1.0, jax.random.fold_in(own_key, 6)
    for dim, shards_of in cuts:
        steps = jnp.exp(jax.random.uniform(jax.random.fold_in(own, dim), (shards_of,), jnp.float32, smallest / len(cuts), top_value / len(cuts)))
        level = level * jnp.repeat(steps, shape[dim] // shards_of).reshape([-1 if axis == dim else 1 for axis in range(len(shape))])
    return level


def bell_draw(stream_key, dims, deviation, reach, shards=(), kind=jnp.bfloat16):
    array = jax.random.normal(stream_key, dims, jnp.float32) * deviation
    if len(shards) > 0:
        array = levels(stream_key, dims, shards, -0.22, 0.18) * array
    return jnp.clip(array, min=-reach, max=reach).astype(kind)


def setup_inputs(seed: int = 0, part: int = 0) -> dict:
    splits = jax.random.split(jax.random.key(seed), 9)
    part_splits = jax.random.split(jax.random.fold_in(splits[8], part), 9)
    tokens = bell_draw(part_splits[0], (TOKENS, D), 1.0, 6.0, ((0, 8),))
    query_weight = bell_draw(splits[1], (D, D), D ** -0.5, 0.15625, ((1, 2),))
    key_weight = bell_draw(splits[2], (D, D), D ** -0.5, 0.15625, ((1, 2),))
    value_weight = bell_draw(splits[3], (D, D), D ** -0.5, 0.15625, ((1, 2),))
    out_weight = bell_draw(splits[4], (D, D), (D // 16) ** -0.5, 0.625, ((0, 2),))
    block_mask = draw_block_mask(jax.random.fold_in(jax.random.fold_in(splits[8], part), 71), part)
    frame_level = plant(jax.random.randint(part_splits[6], (FRAMES,), 0, LEVELS), jax.random.fold_in(part_splits[6], 1), 0, LEVELS - 1).astype(jnp.int32)
    modulation = draw_modulation(jax.random.fold_in(splits[8], 71), part)
    return {"tokens": tokens, "query_weight": query_weight, "key_weight": key_weight, "value_weight": value_weight, "out_weight": out_weight, "block_mask": block_mask, "frame_level": frame_level, "modulation": modulation}


def visible(span_index, span_len, total_keys):
    key_place = jnp.arange(total_keys, dtype=jnp.int32)
    near_start = SINK + span_len
    own_start = SINK + 2 * span_len
    return (key_place < SINK) | (key_place >= own_start) | (key_place >= near_start) & (span_index >= 1) | (key_place < near_start) & (span_index >= 2)

def reference(tokens, query_weight, key_weight, value_weight, out_weight, block_mask, frame_level, modulation):
    xfloat = tokens.astype(jnp.float32)
    mean_square = lax.optimization_barrier(jnp.mean(xfloat * xfloat, axis=-1, keepdims=True))
    normed = xfloat * lax.rsqrt(mean_square + 1e-06)
    chosen = modulation[frame_level]
    shaped = normed.reshape(FRAMES, FRAME_TOK, D)
    modulated = (shaped * (1.0 + chosen[:, None, 0]) + chosen[:, None, 1]).reshape(TOKENS, D).astype(jnp.bfloat16)
    score_scale = 1.0 / math.sqrt(HEAD_DIM)
    query_all = (jnp.dot(modulated, query_weight, preferred_element_type=jnp.float32) * score_scale).astype(jnp.bfloat16).reshape(SPANS, SPAN, HEADS, HEAD_DIM)
    key_all = jnp.dot(modulated, key_weight, preferred_element_type=jnp.float32).astype(jnp.bfloat16).reshape(SPANS, SPAN, HEADS, HEAD_DIM)
    value_all = jnp.dot(modulated, value_weight, preferred_element_type=jnp.float32).astype(jnp.bfloat16).reshape(SPANS, SPAN, HEADS, HEAD_DIM)
    sink_keys = key_all[0, :SINK]
    sink_values = value_all[0, :SINK]

    def one_span(span_index):
        earlier = jnp.maximum(span_index - 2, 0)
        previous = jnp.maximum(span_index - 1, 0)
        key_rows = jnp.concatenate([sink_keys, key_all[earlier], key_all[previous], key_all[span_index]], axis=0)
        value_rows = jnp.concatenate([sink_values, value_all[earlier], value_all[previous], value_all[span_index]], axis=0)
        tile_mask = block_mask[span_index]
        tile_full = jnp.broadcast_to(tile_mask[:, None, :, None], (QBLOCKS, TILE, KBLOCKS, TILE)).reshape(SPAN, KEYS)
        allowed = (tile_full > 0) & visible(span_index, SPAN, KEYS)[None, :]
        score_rows = jnp.einsum('qhd,khd->hqk', query_all[span_index].astype(jnp.float32), key_rows.astype(jnp.float32))
        masked_scores = jnp.where(allowed[None], score_rows, -1e+30)
        row_peak = lax.optimization_barrier(jnp.max(masked_scores, axis=-1, keepdims=True))
        softmax_num = jnp.where(allowed[None], jnp.exp(masked_scores - row_peak), 0.0)
        row_total = lax.optimization_barrier(jnp.sum(softmax_num, axis=-1))
        weights_bf = lax.optimization_barrier(softmax_num.astype(jnp.bfloat16))
        mixed_rows = jnp.einsum('hqk,khd->qhd', weights_bf.astype(jnp.float32), value_rows.astype(jnp.float32))
        return (mixed_rows / row_total.T[:, :, None]).astype(jnp.bfloat16).reshape(SPAN, D)
    attention_out = lax.map(one_span, jnp.arange(SPANS, dtype=jnp.int32)).reshape(TOKENS, D)
    return (xfloat + jnp.dot(attention_out, out_weight, preferred_element_type=jnp.float32)).astype(jnp.bfloat16)
```

```python
import functools
import math

import jax
import jax.numpy as jnp
from jax import lax
from jax.experimental import pallas as pl
from jax.experimental.pallas import tpu as pltpu
from jax.sharding import PartitionSpec as P

HEAD_DIM = 128
FRAME_TOK = 128
SINK = 128
TILE = 128
CHUNK = 64
DIRECT = 5
MESH = pl.DeviceIdType.MESH


def layer_kernel(
    frames,
    tok_hbm,
    wq_hbm,
    wk_hbm,
    wv_hbm,
    wo_hbm,
    mask_ref,
    level_ref,
    table_ref,
    out_ref,
    tok,
    resid,
    wq,
    wk,
    wv,
    wo_mine,
    wo_theirs,
    own,
    far,
    near,
    sink,
    qbuf,
    kbuf,
    vbuf,
    outgoing,
    incoming,
    kept,
    load_sem,
    sz,
    sy,
    sxf,
    sxn,
    ss,
    rf,
    rn,
    rs,
    so,
    ro,
):
    c = lax.axis_index("frame")
    h = lax.axis_index("head")
    chunks, rows, width = own.shape
    local = wq.shape[1]
    share = out_ref.shape[1]
    heads = local // HEAD_DIM
    span = chunks * rows
    relays = chunks - DIRECT
    even = c % 2 == 0
    total_keys = kbuf.shape[0]
    far_start, near_start, own_start = SINK, SINK + span, SINK + 2 * span

    def load(src, dst, i):
        return pltpu.make_async_copy(src, dst, load_sem.at[i])

    my_cols = pl.ds(pl.multiple_of(h * share, share), share)
    their_cols = pl.ds(pl.multiple_of((1 - h) * share, share), share)
    loads = [
        load(tok_hbm, tok, 0),
        load(wq_hbm, wq, 1),
        load(wk_hbm, wk, 2),
        load(wv_hbm, wv, 3),
        load(wo_hbm.at[:, their_cols], wo_theirs, 4),
        load(wo_hbm.at[:, my_cols], wo_mine, 5),
        load(tok_hbm.at[:, my_cols], resid, 6),
    ]
    for one in loads:
        one.start()

    barrier = pltpu.get_barrier_semaphore()
    pl.semaphore_signal(barrier, inc=1, device_id={"head": 1 - h}, device_id_type=MESH)
    expected = 1
    for step in (1, 2):
        for there, valid in ((c - step, c >= step), (c + step, c + step < frames)):

            @pl.when(valid)
            def _():
                pl.semaphore_signal(
                    barrier, inc=1, device_id={"frame": there}, device_id_type=MESH
                )

            expected = expected + jnp.where(valid, 1, 0)
    pl.semaphore_wait(barrier, expected)

    def place(k):
        return jnp.where(h == 0, k, chunks - 1 - k)

    def remote(src, dst, send, recv, device):
        return pltpu.make_async_remote_copy(
            src_ref=src,
            dst_ref=dst,
            send_sem=send,
            recv_sem=recv,
            device_id=device,
            device_id_type=MESH,
        )

    def z_copy(k):
        i = place(k)
        return remote(own.at[i], far.at[i], sz.at[k], rf.at[i], {"frame": c + 2})

    def y_copy_even(k):
        i = place(k)
        return remote(own.at[i], near.at[i], sy.at[k], rn.at[i], {"frame": c + 1})

    def y_copy_odd(k):
        i = place(k)
        return remote(far.at[i], near.at[i], sy.at[k], rn.at[i], {"frame": c - 1})

    def x_copy_far(k):
        i = place(k)
        return remote(far.at[i], far.at[i], sxf.at[k], rf.at[i], {"head": 1 - h})

    def x_copy_near(k):
        i = place(k)
        return remote(near.at[i], near.at[i], sxn.at[k], rn.at[i], {"head": 1 - h})

    def sink_copy(n, device):
        return remote(sink.at[h], sink.at[h], ss.at[n], rs.at[h], device)

    sink_z = lambda: sink_copy(0, {"frame": c + 2})
    sink_y = lambda: sink_copy(1, {"frame": c + 1})
    sink_x = lambda: sink_copy(2, {"head": 1 - h})
    has_z = c + 2 < frames
    has_far = c >= 2
    has_near = c >= 1

    def modulate(i):
        x = tok[pl.ds(pl.multiple_of(i * rows, rows), rows), :].astype(jnp.float32)
        mean_square = jnp.mean(x * x, axis=-1, keepdims=True)
        normed = x * lax.rsqrt(mean_square + 1e-06)
        level = level_ref[i // (FRAME_TOK // rows)]
        scale_shift = table_ref[level]
        return (normed * (1.0 + scale_shift[0:1]) + scale_shift[1:2]).astype(jnp.bfloat16)

    def send_own(k):
        @pl.when(has_z)
        def _():
            z_copy(k).start()

        @pl.when(even)
        def _():
            y_copy_even(k).start()

    def sink_forward(lo, hi):
        @pl.when((c >= lo) & (c < hi))
        def _():
            sink_z().wait_recv()
            sink_x().start()

            @pl.when(even & has_z)
            def _():
                sink_z().start()

            @pl.when(even)
            def _():
                sink_y().start()

    def far_arrive(k):
        @pl.when(has_far)
        def _():
            z_copy(k).wait_recv()
            if k < relays:
                x_copy_far(k).start()

            @pl.when(jnp.logical_not(even))
            def _():
                y_copy_odd(k).start()

    def near_arrive(k):
        @pl.when(has_near)
        def _():
            y_copy_even(k).wait_recv()
            if k < relays:
                x_copy_near(k).start()

    loads[0].wait()

    @pl.when(c == 0)
    def _():
        for i in range(SINK // rows):
            sink[i] = modulate(i)

        @pl.when(has_z)
        def _():
            sink_z().start()

        sink_y().start()

    early = 2
    for k in range(early):
        own[place(k)] = modulate(place(k))
        send_own(k)

    def rest(k, carry):
        own[place(k)] = modulate(place(k))
        return carry

    lax.fori_loop(early, chunks, rest, 0)

    col_tile = 256

    def project(src, weight, dst, start, count, scale=None):
        flat = src[...].reshape(count, width)

        def tile(n, carry):
            cols = pl.ds(pl.multiple_of(n * col_tile, col_tile), col_tile)
            res = jnp.dot(flat, weight[:, cols], preferred_element_type=jnp.float32)
            if scale is not None:
                res = res * scale
            dst[start : start + count, cols] = res.astype(jnp.bfloat16)
            return carry

        lax.fori_loop(0, local // col_tile, tile, 0)

    loads[1].wait()
    project(own, wq, qbuf, 0, span, 1.0 / math.sqrt(HEAD_DIM))

    sink_forward(1, 3)
    send_own(2)
    far_arrive(0)

    loads[2].wait()
    project(own, wk, kbuf, own_start, span)
    loads[3].wait()
    project(own, wv, vbuf, own_start, span)

    sink_forward(3, 5)
    for k in range(3, DIRECT):
        send_own(k)
    far_arrive(1)
    near_arrive(0)
    far_arrive(2)
    near_arrive(1)
    far_arrive(3)
    near_arrive(2)
    sink_forward(5, frames)
    far_arrive(4)
    near_arrive(3)
    near_arrive(4)

    @pl.when(has_far)
    def _():
        for k in range(DIRECT, chunks):
            remote(
                far.at[place(k)], far.at[place(k)], sxf.at[0], rf.at[place(k)], {"head": 1 - h}
            ).wait_recv()
        project(far, wk, kbuf, far_start, span)
        project(far, wv, vbuf, far_start, span)

    @pl.when(jnp.logical_not(has_far))
    def _():
        kbuf[far_start:near_start, :] = jnp.zeros((span, local), jnp.bfloat16)
        vbuf[far_start:near_start, :] = jnp.zeros((span, local), jnp.bfloat16)

    @pl.when(has_near)
    def _():
        remote(sink.at[1 - h], sink.at[1 - h], ss.at[2], rs.at[1 - h], {"head": 1 - h}).wait_recv()

    project(sink, wk, kbuf, 0, SINK)
    project(sink, wv, vbuf, 0, SINK)

    @pl.when(has_near)
    def _():
        for k in range(DIRECT, chunks):
            remote(
                near.at[place(k)], near.at[place(k)], sxn.at[0], rn.at[place(k)], {"head": 1 - h}
            ).wait_recv()
        project(near, wk, kbuf, near_start, span)
        project(near, wv, vbuf, near_start, span)

    @pl.when(jnp.logical_not(has_near))
    def _():
        kbuf[near_start:own_start, :] = jnp.zeros((span, local), jnp.bfloat16)
        vbuf[near_start:own_start, :] = jnp.zeros((span, local), jnp.bfloat16)

    for i in (4, 5, 6):
        loads[i].wait()

    key_blocks = total_keys // TILE
    far_ok = jnp.where(has_far, 1, 0)
    near_ok = jnp.where(has_near, 1, 0)

    def out_copy(b):
        return remote(outgoing.at[b], incoming.at[b], so.at[b], ro.at[b], {"head": 1 - h})

    def query_block(b, carry):
        q_rows = pl.ds(pl.multiple_of(b * TILE, TILE), TILE)
        parts = []
        for j in range(key_blocks):
            seen = mask_ref[b, j]
            if far_start <= j * TILE < near_start:
                seen = seen * far_ok
            elif near_start <= j * TILE < own_start:
                seen = seen * near_ok
            parts.append(jnp.full((1, TILE), jnp.where(seen > 0, 0.0, -1e30), jnp.float32))
        bias = jnp.concatenate(parts, axis=1)
        mixed = []
        for n in range(heads):
            cols = slice(n * HEAD_DIM, (n + 1) * HEAD_DIM)
            scores = lax.dot_general(
                qbuf[q_rows, cols],
                kbuf[:, cols],
                (((1,), (1,)), ((), ())),
                preferred_element_type=jnp.float32,
            )
            scores = scores + bias
            peak = jnp.max(scores, axis=-1, keepdims=True)
            num = jnp.exp(scores - peak)
            total = jnp.sum(num, axis=-1, keepdims=True)
            rows_out = jnp.dot(
                num.astype(jnp.bfloat16), vbuf[:, cols], preferred_element_type=jnp.float32
            )
            mixed.append((rows_out / total).astype(jnp.bfloat16))
        attended = jnp.concatenate(mixed, axis=1)
        outgoing[b] = jnp.dot(
            attended, wo_theirs[...], preferred_element_type=jnp.float32
        ).astype(jnp.bfloat16)
        out_copy(b).start()
        kept[b] = resid[q_rows, :].astype(jnp.float32) + jnp.dot(
            attended, wo_mine[...], preferred_element_type=jnp.float32
        )
        return carry

    blocks = span // TILE
    lax.fori_loop(0, blocks, query_block, 0)

    def finish(b, carry):
        q_rows = pl.ds(pl.multiple_of(b * TILE, TILE), TILE)
        out_copy(b).wait_recv()
        out_ref[q_rows, :] = (kept[b] + incoming[b].astype(jnp.float32)).astype(jnp.bfloat16)
        return carry

    lax.fori_loop(0, blocks, finish, 0)

    def finish_send(b, carry):
        out_copy(b).wait_send()
        return carry

    lax.fori_loop(0, blocks, finish_send, 0)

    for k in range(DIRECT):

        @pl.when(has_z)
        def _():
            z_copy(k).wait_send()

        @pl.when(even)
        def _():
            y_copy_even(k).wait_send()

        @pl.when(jnp.logical_not(even) & has_far)
        def _():
            y_copy_odd(k).wait_send()

    for k in range(relays):

        @pl.when(has_far)
        def _():
            x_copy_far(k).wait_send()

        @pl.when(has_near)
        def _():
            x_copy_near(k).wait_send()

    @pl.when(even & has_z)
    def _():
        sink_z().wait_send()

    @pl.when(even)
    def _():
        sink_y().wait_send()

    @pl.when(has_near)
    def _():
        sink_x().wait_send()


def shards(
    tokens, query_weight, key_weight, value_weight, out_weight, block_mask, frame_level, modulation
):
    span, width = tokens.shape
    local = query_weight.shape[1]
    share = width // lax.axis_size("head")
    chunks = span // CHUNK
    relays = chunks - DIRECT
    blocks = span // TILE
    total_keys = SINK + 3 * span
    bf16, f32 = jnp.bfloat16, jnp.float32
    dma = pltpu.SemaphoreType.DMA
    anywhere = pl.BlockSpec(memory_space=pl.ANY)
    smem = pl.BlockSpec(memory_space=pltpu.SMEM)
    vmem = pl.BlockSpec(memory_space=pltpu.VMEM)
    return pl.pallas_call(
        functools.partial(layer_kernel, lax.axis_size("frame")),
        out_shape=jax.ShapeDtypeStruct((span, share), bf16),
        in_specs=[anywhere] * 5 + [smem, smem, vmem],
        out_specs=vmem,
        scratch_shapes=[
            pltpu.VMEM((span, width), bf16),
            pltpu.VMEM((span, share), bf16),
            pltpu.VMEM((width, local), bf16),
            pltpu.VMEM((width, local), bf16),
            pltpu.VMEM((width, local), bf16),
            pltpu.VMEM((local, share), bf16),
            pltpu.VMEM((local, share), bf16),
            pltpu.VMEM((chunks, CHUNK, width), bf16),
            pltpu.VMEM((chunks, CHUNK, width), bf16),
            pltpu.VMEM((chunks, CHUNK, width), bf16),
            pltpu.VMEM((SINK // CHUNK, CHUNK, width), bf16),
            pltpu.VMEM((span, local), bf16),
            pltpu.VMEM((total_keys, local), bf16),
            pltpu.VMEM((total_keys, local), bf16),
            pltpu.VMEM((blocks, TILE, share), bf16),
            pltpu.VMEM((blocks, TILE, share), bf16),
            pltpu.VMEM((blocks, TILE, share), f32),
            dma((7,)),
            dma((DIRECT,)),
            dma((DIRECT,)),
            dma((relays,)),
            dma((relays,)),
            dma((3,)),
            dma((chunks,)),
            dma((chunks,)),
            dma((2,)),
            dma((blocks,)),
            dma((blocks,)),
        ],
        compiler_params=pltpu.CompilerParams(
            collective_id=0, has_side_effects=True, vmem_limit_bytes=60 * 1024 * 1024
        ),
        name="layer",
    )(
        tokens,
        query_weight,
        key_weight,
        value_weight,
        out_weight,
        block_mask[0],
        frame_level,
        modulation,
    )


def solution(mesh):
    placed = (
        P(("batch", "frame"), None),
        P(None, "head"),
        P(None, "head"),
        P(None, "head"),
        P("head", None),
        P(("batch", "frame"), None, None),
        P(("batch", "frame")),
        P(),
    )
    return jax.shard_map(
        shards, mesh=mesh, in_specs=placed, out_specs=P(("batch", "frame"), "head"), check_vma=False
    )
```

```python
import functools
import math

import jax
import jax.numpy as jnp
from jax import lax
from jax.experimental import pallas as pl
from jax.experimental.pallas import tpu as pltpu
from jax.sharding import PartitionSpec as P

HEAD_DIM = 128
FRAME_TOK = 128
SINK = 128
TILE = 128
CHUNK = 64
DIRECT = 6
MESH = pl.DeviceIdType.MESH


def layer_kernel(
    frames,
    tok_hbm,
    wq_hbm,
    wk_hbm,
    wv_hbm,
    wo_hbm,
    mask_ref,
    level_ref,
    table_ref,
    out_ref,
    tok,
    resid,
    wq,
    wk,
    wv,
    wo_mine,
    wo_theirs,
    own,
    far,
    near,
    sink,
    qbuf,
    kbuf,
    vbuf,
    outgoing,
    incoming,
    kept,
    load_sem,
    sz,
    sy,
    sxf,
    sxn,
    ss,
    rf,
    rn,
    rs,
    so,
    ro,
):
    c = lax.axis_index("frame")
    h = lax.axis_index("head")
    chunks, rows, width = own.shape
    local = wq.shape[1]
    share = out_ref.shape[1]
    heads = local // HEAD_DIM
    span = chunks * rows
    relays = chunks - DIRECT
    even = c % 2 == 0
    total_keys = kbuf.shape[0]
    far_start, near_start, own_start = SINK, SINK + span, SINK + 2 * span

    def load(src, dst, i):
        return pltpu.make_async_copy(src, dst, load_sem.at[i])

    my_cols = pl.ds(pl.multiple_of(h * share, share), share)
    their_cols = pl.ds(pl.multiple_of((1 - h) * share, share), share)
    loads = [
        load(tok_hbm, tok, 0),
        load(wq_hbm, wq, 1),
        load(wk_hbm, wk, 2),
        load(wv_hbm, wv, 3),
        load(wo_hbm.at[:, their_cols], wo_theirs, 4),
        load(wo_hbm.at[:, my_cols], wo_mine, 5),
        load(tok_hbm.at[:, my_cols], resid, 6),
    ]
    for one in loads:
        one.start()

    barrier = pltpu.get_barrier_semaphore()
    pl.semaphore_signal(barrier, inc=1, device_id={"head": 1 - h}, device_id_type=MESH)
    expected = 1
    for step in (1, 2):
        for there, valid in ((c - step, c >= step), (c + step, c + step < frames)):

            @pl.when(valid)
            def _():
                pl.semaphore_signal(
                    barrier, inc=1, device_id={"frame": there}, device_id_type=MESH
                )

            expected = expected + jnp.where(valid, 1, 0)
    pl.semaphore_wait(barrier, expected)

    def place(k):
        return jnp.where(h == 0, k, chunks - 1 - k)

    def remote(src, dst, send, recv, device):
        return pltpu.make_async_remote_copy(
            src_ref=src,
            dst_ref=dst,
            send_sem=send,
            recv_sem=recv,
            device_id=device,
            device_id_type=MESH,
        )

    def z_copy(k):
        i = place(k)
        return remote(own.at[i], far.at[i], sz.at[k], rf.at[i], {"frame": c + 2})

    def y_copy_even(k):
        i = place(k)
        return remote(own.at[i], near.at[i], sy.at[k], rn.at[i], {"frame": c + 1})

    def y_copy_odd(k):
        i = place(k)
        return remote(far.at[i], near.at[i], sy.at[k], rn.at[i], {"frame": c - 1})

    def x_copy_far(k):
        i = place(k)
        return remote(far.at[i], far.at[i], sxf.at[k], rf.at[i], {"head": 1 - h})

    def x_copy_near(k):
        i = place(k)
        return remote(near.at[i], near.at[i], sxn.at[k], rn.at[i], {"head": 1 - h})

    def sink_copy(n, device):
        return remote(sink.at[h], sink.at[h], ss.at[n], rs.at[h], device)

    sink_z = lambda: sink_copy(0, {"frame": c + 2})
    sink_y = lambda: sink_copy(1, {"frame": c + 1})
    sink_x = lambda: sink_copy(2, {"head": 1 - h})
    has_z = c + 2 < frames
    has_far = c >= 2
    has_near = c >= 1

    def modulate(i):
        x = tok[pl.ds(pl.multiple_of(i * rows, rows), rows), :].astype(jnp.float32)
        mean_square = jnp.mean(x * x, axis=-1, keepdims=True)
        normed = x * lax.rsqrt(mean_square + 1e-06)
        level = level_ref[i // (FRAME_TOK // rows)]
        scale_shift = table_ref[level]
        return (normed * (1.0 + scale_shift[0:1]) + scale_shift[1:2]).astype(jnp.bfloat16)

    def send_own(k):
        @pl.when(has_z)
        def _():
            z_copy(k).start()

        @pl.when(even)
        def _():
            y_copy_even(k).start()

    def sink_even(lo, hi):
        @pl.when(even & (c >= lo) & (c < hi))
        def _():
            sink_z().wait_recv()
            sink_x().start()
            sink_y().start()

            @pl.when(has_z)
            def _():
                sink_z().start()

    def sink_odd():
        @pl.when(jnp.logical_not(even))
        def _():
            sink_z().wait_recv()
            sink_x().start()

    def far_arrive(k):
        @pl.when(has_far)
        def _():
            z_copy(k).wait_recv()
            if k < relays:
                x_copy_far(k).start()

            @pl.when(jnp.logical_not(even))
            def _():
                y_copy_odd(k).start()

    def near_arrive(k):
        @pl.when(has_near)
        def _():
            y_copy_even(k).wait_recv()
            if k < relays:
                x_copy_near(k).start()

    loads[0].wait()

    @pl.when(c == 0)
    def _():
        for i in range(SINK // rows):
            sink[i] = modulate(i)

        @pl.when(has_z)
        def _():
            sink_z().start()

        sink_y().start()

    early = 2
    for k in range(early):
        own[place(k)] = modulate(place(k))
        send_own(k)

    def rest(k, carry):
        own[place(k)] = modulate(place(k))
        return carry

    lax.fori_loop(early, chunks, rest, 0)

    col_tile = 256

    def project(src, weight, dst, start, scale=None):
        flat = src[...].reshape(-1, width)
        count = flat.shape[0]
        if not isinstance(start, int):
            start = pl.multiple_of(start, TILE)

        def tile(n, carry):
            cols = pl.ds(pl.multiple_of(n * col_tile, col_tile), col_tile)
            res = jnp.dot(flat, weight[:, cols], preferred_element_type=jnp.float32)
            if scale is not None:
                res = res * scale
            dst[pl.ds(start, count), cols] = res.astype(jnp.bfloat16)
            return carry

        lax.fori_loop(0, local // col_tile, tile, 0)

    half = chunks // 2

    def project_half(src, start, which):
        piece = src.at[pl.ds(which * half, half)]
        project(piece, wk, kbuf, start + which * half * rows)
        project(piece, wv, vbuf, start + which * half * rows)

    def relayed_wait(buf, send, recv):
        for k in range(DIRECT, chunks):
            i = place(k)
            remote(buf.at[i], buf.at[i], send.at[0], recv.at[i], {"head": 1 - h}).wait_recv()

    loads[1].wait()
    project(own, wq, qbuf, 0, 1.0 / math.sqrt(HEAD_DIM))

    sink_even(2, 3)
    send_own(2)
    far_arrive(0)

    loads[2].wait()
    project(own, wk, kbuf, own_start)
    loads[3].wait()
    project(own, wv, vbuf, own_start)

    sink_even(4, 5)
    send_own(3)
    far_arrive(1)
    near_arrive(0)
    far_arrive(2)
    near_arrive(1)
    sink_even(6, frames)
    for k in range(4, DIRECT):
        send_own(k)
    far_arrive(3)
    near_arrive(2)

    @pl.when(has_far)
    def _():
        project_half(far, far_start, h)

    @pl.when(jnp.logical_not(has_far))
    def _():
        kbuf[far_start:near_start, :] = jnp.zeros((span, local), jnp.bfloat16)
        vbuf[far_start:near_start, :] = jnp.zeros((span, local), jnp.bfloat16)

    far_arrive(4)
    near_arrive(3)

    @pl.when(has_near)
    def _():
        project_half(near, near_start, h)

    @pl.when(jnp.logical_not(has_near))
    def _():
        kbuf[near_start:own_start, :] = jnp.zeros((span, local), jnp.bfloat16)
        vbuf[near_start:own_start, :] = jnp.zeros((span, local), jnp.bfloat16)

    sink_odd()
    far_arrive(5)
    near_arrive(4)

    @pl.when(has_far)
    def _():
        relayed_wait(far, sxf, rf)
        project_half(far, far_start, 1 - h)

    @pl.when(has_near)
    def _():
        remote(sink.at[1 - h], sink.at[1 - h], ss.at[2], rs.at[1 - h], {"head": 1 - h}).wait_recv()

    project(sink, wk, kbuf, 0)
    project(sink, wv, vbuf, 0)
    near_arrive(5)

    @pl.when(has_near)
    def _():
        relayed_wait(near, sxn, rn)
        project_half(near, near_start, 1 - h)

    for i in (4, 5, 6):
        loads[i].wait()

    key_blocks = total_keys // TILE
    far_ok = jnp.where(has_far, 1, 0)
    near_ok = jnp.where(has_near, 1, 0)

    def out_copy(b):
        return remote(outgoing.at[b], incoming.at[b], so.at[b], ro.at[b], {"head": 1 - h})

    def query_block(b, carry):
        q_rows = pl.ds(pl.multiple_of(b * TILE, TILE), TILE)
        parts = []
        for j in range(key_blocks):
            seen = mask_ref[b, j]
            if far_start <= j * TILE < near_start:
                seen = seen * far_ok
            elif near_start <= j * TILE < own_start:
                seen = seen * near_ok
            parts.append(jnp.full((1, TILE), jnp.where(seen > 0, 0.0, -1e30), jnp.float32))
        bias = jnp.concatenate(parts, axis=1)
        mixed = []
        for n in range(heads):
            cols = slice(n * HEAD_DIM, (n + 1) * HEAD_DIM)
            scores = lax.dot_general(
                qbuf[q_rows, cols],
                kbuf[:, cols],
                (((1,), (1,)), ((), ())),
                preferred_element_type=jnp.float32,
            )
            scores = scores + bias
            peak = jnp.max(scores, axis=-1, keepdims=True)
            num = jnp.exp(scores - peak)
            total = jnp.sum(num, axis=-1, keepdims=True)
            rows_out = jnp.dot(
                num.astype(jnp.bfloat16), vbuf[:, cols], preferred_element_type=jnp.float32
            )
            mixed.append((rows_out / total).astype(jnp.bfloat16))
        attended = jnp.concatenate(mixed, axis=1)
        outgoing[b] = jnp.dot(
            attended, wo_theirs[...], preferred_element_type=jnp.float32
        ).astype(jnp.bfloat16)
        out_copy(b).start()
        kept[b] = resid[q_rows, :].astype(jnp.float32) + jnp.dot(
            attended, wo_mine[...], preferred_element_type=jnp.float32
        )
        return carry

    blocks = span // TILE
    lax.fori_loop(0, blocks, query_block, 0)

    def finish(b, carry):
        q_rows = pl.ds(pl.multiple_of(b * TILE, TILE), TILE)
        out_copy(b).wait_recv()
        out_ref[q_rows, :] = (kept[b] + incoming[b].astype(jnp.float32)).astype(jnp.bfloat16)
        return carry

    lax.fori_loop(0, blocks, finish, 0)

    def finish_send(b, carry):
        out_copy(b).wait_send()
        return carry

    lax.fori_loop(0, blocks, finish_send, 0)

    for k in range(DIRECT):

        @pl.when(has_z)
        def _():
            z_copy(k).wait_send()

        @pl.when(even)
        def _():
            y_copy_even(k).wait_send()

        @pl.when(jnp.logical_not(even) & has_far)
        def _():
            y_copy_odd(k).wait_send()

    for k in range(relays):

        @pl.when(has_far)
        def _():
            x_copy_far(k).wait_send()

        @pl.when(has_near)
        def _():
            x_copy_near(k).wait_send()

    @pl.when(even & has_z)
    def _():
        sink_z().wait_send()

    @pl.when(even)
    def _():
        sink_y().wait_send()

    @pl.when(has_near)
    def _():
        sink_x().wait_send()


def shards(
    tokens, query_weight, key_weight, value_weight, out_weight, block_mask, frame_level, modulation
):
    span, width = tokens.shape
    local = query_weight.shape[1]
    share = width // lax.axis_size("head")
    chunks = span // CHUNK
    relays = chunks - DIRECT
    blocks = span // TILE
    total_keys = SINK + 3 * span
    bf16, f32 = jnp.bfloat16, jnp.float32
    dma = pltpu.SemaphoreType.DMA
    anywhere = pl.BlockSpec(memory_space=pl.ANY)
    smem = pl.BlockSpec(memory_space=pltpu.SMEM)
    vmem = pl.BlockSpec(memory_space=pltpu.VMEM)
    return pl.pallas_call(
        functools.partial(layer_kernel, lax.axis_size("frame")),
        out_shape=jax.ShapeDtypeStruct((span, share), bf16),
        in_specs=[anywhere] * 5 + [smem, smem, vmem],
        out_specs=vmem,
        scratch_shapes=[
            pltpu.VMEM((span, width), bf16),
            pltpu.VMEM((span, share), bf16),
            pltpu.VMEM((width, local), bf16),
            pltpu.VMEM((width, local), bf16),
            pltpu.VMEM((width, local), bf16),
            pltpu.VMEM((local, share), bf16),
            pltpu.VMEM((local, share), bf16),
            pltpu.VMEM((chunks, CHUNK, width), bf16),
            pltpu.VMEM((chunks, CHUNK, width), bf16),
            pltpu.VMEM((chunks, CHUNK, width), bf16),
            pltpu.VMEM((SINK // CHUNK, CHUNK, width), bf16),
            pltpu.VMEM((span, local), bf16),
            pltpu.VMEM((total_keys, local), bf16),
            pltpu.VMEM((total_keys, local), bf16),
            pltpu.VMEM((blocks, TILE, share), bf16),
            pltpu.VMEM((blocks, TILE, share), bf16),
            pltpu.VMEM((blocks, TILE, share), f32),
            dma((7,)),
            dma((DIRECT,)),
            dma((DIRECT,)),
            dma((relays,)),
            dma((relays,)),
            dma((3,)),
            dma((chunks,)),
            dma((chunks,)),
            dma((2,)),
            dma((blocks,)),
            dma((blocks,)),
        ],
        compiler_params=pltpu.CompilerParams(
            collective_id=0, has_side_effects=True, vmem_limit_bytes=60 * 1024 * 1024
        ),
        name="layer",
    )(
        tokens,
        query_weight,
        key_weight,
        value_weight,
        out_weight,
        block_mask[0],
        frame_level,
        modulation,
    )


def solution(mesh):
    placed = (
        P(("batch", "frame"), None),
        P(None, "head"),
        P(None, "head"),
        P(None, "head"),
        P("head", None),
        P(("batch", "frame"), None, None),
        P(("batch", "frame")),
        P(),
    )
    return jax.shard_map(
        shards, mesh=mesh, in_specs=placed, out_specs=P(("batch", "frame"), "head"), check_vma=False
    )
```
